32 devices in a mesh: rows: 8 (over z, core), ch: 4 (over y, x).
Axes of the slice: x: 2, y: 2, z: 4, core: 2. Of those that a mesh axis runs over, the one named last changes fastest.
Arguments:
- features: bfloat16 [32, 256, 2048], P('rows', None, 'ch'), may hold values from -6 to 6
- conv_weight: bfloat16 [3, 3, 256, 256], P(None, None, 'ch'), may hold values from -0.125 to 0.125
- cotangent: bfloat16 [32, 256, 2048], P('rows', None, 'ch'), may hold values from -6 to 6
- valid_rows: int32 [16], replicated, may hold values from 16 to 32
Outputs:
- input_grad: bfloat16 [32, 256, 2048], P('rows', None, 'ch')
- weight_grad: float32 [3, 3, 256, 256], P(None, None, 'ch')
The draws below stay inside these ranges and needn't reach their ends.
All inputs are finite; a program needn't handle non-finite values.
Results may differ from the reference program's by a relative error of at most 0.0049.
Values may be sent and summed in bfloat16 or wider, within the bound.
A program may use at most 64 MiB of HBM per device.

```python
import jax
import jax.numpy as jnp
from jax import lax

C = 256
COLS = 128
IMAGES = 16
H = 32


def place_ends(drawn, own_key, low, top_value):
    extent = drawn.shape
    place = [jax.random.randint(jax.random.fold_in(own_key, axis), (), 0, extent[axis]) for axis in range(len(extent))]
    drawn = drawn.at[tuple(place)].set(low)
    longest = extent.index(max(extent))
    place[longest] = (place[longest] + 1) % extent[longest]
    return drawn.at[tuple(place)].set(top_value)


def block_levels(own_key, dims, cuts, low, high):
    def one(dim, parts):
        steps = jax.random.uniform(jax.random.fold_in(jax.random.fold_in(own_key, 6), dim), (parts,), jnp.float32, low / len(cuts), high / len(cuts))
        return jnp.repeat(jnp.exp(steps), dims[dim] // parts).reshape((-1,) + (1,) * (len(dims) - dim - 1))

    gain = one(*cuts[0])
    for cut in cuts[1:]:
        gain = gain * one(*cut)
    return gain


def scatter_about(own_key, shape, scale, bound, cuts=(), kind=jnp.bfloat16):
    result = jax.random.normal(own_key, shape, jnp.float32) * scale
    if len(cuts) > 0:
        result = block_levels(own_key, shape, cuts, -0.22, 0.18) * result
    return jnp.clip(result, min=-bound, max=bound).astype(kind)


def setup_inputs(seed: int = 0) -> dict:
    key_of = jax.random.split(jax.random.key(seed), 5)
    return {
        "features": scatter_about(key_of[0], (H, C, IMAGES * COLS), 1.0, 6.0, ((0, 8), (2, 4))),
        "conv_weight": scatter_about(key_of[1], (3, 3, C, C), (9 * C) ** -0.5, 0.125, ((2, 4),)),
        "cotangent": scatter_about(key_of[2], (H, C, IMAGES * COLS), 1.0, 6.0, ((0, 8), (2, 4))),
        "valid_rows": place_ends(jax.random.randint(key_of[3], (IMAGES,), H // 2, H + 1), jax.random.fold_in(key_of[3], 1), H // 2, H).astype(jnp.int32),
    }


def shift_cols(field, across, columns):
    if across == 0:
        return field
    length = field.shape[-1]
    widths = [(0, 0)] * (field.ndim - 1) + [(1, 1)]
    padded = jnp.pad(field, widths)
    moved = padded[..., 1 + across:1 + across + length]
    position = jnp.arange(length).astype(jnp.int32) % columns + across
    inside = (position >= 0) & (position < columns)
    return jnp.where(inside, moved, jnp.zeros_like(moved))

def shifted(field, down, across, columns):
    height = field.shape[0]
    widths = [(1, 1)] + [(0, 0)] * (field.ndim - 1)
    padded = jnp.pad(field, widths)
    return shift_cols(padded[1 + down:1 + down + height], across, columns)

def reference(features, conv_weight, cotangent, valid_rows):
    kernel = conv_weight.astype(jnp.float32)
    feat_images = features.reshape((H, C, IMAGES, COLS)).transpose((2, 0, 1, 3))
    cot_images = cotangent.reshape((H, C, IMAGES, COLS)).transpose((2, 0, 1, 3))

    def per_image(carry, item):
        feat, cot, limit = item
        inputs = feat.astype(jnp.float32)
        summed = jnp.zeros(inputs.shape, jnp.float32)
        for offset_row in range(3):
            for offset_col in range(3):
                summed = summed + jnp.einsum('hik,oi->hok', shifted(inputs, offset_row - 1, offset_col - 1, COLS), kernel[offset_row, offset_col])
        center = lax.optimization_barrier(jnp.sum(summed, 1)) / C
        spread = lax.optimization_barrier(jnp.sum(summed * summed, 1)) / C - center * center
        inverse = lax.rsqrt(spread + 1e-06)
        normed = (summed - center[:, None, :]) * inverse[:, None, :]
        row_ids = jnp.arange(H).astype(jnp.int32)
        keep = (row_ids < limit).astype(jnp.float32)
        masked = cot.astype(jnp.float32) * keep[:, None, None]
        grad_mean = lax.optimization_barrier(jnp.sum(masked, 1)) / C
        grad_cross = lax.optimization_barrier(jnp.sum(masked * normed, 1)) / C
        grad_pre = (inverse[:, None, :] * (masked - grad_mean[:, None, :] - normed * grad_cross[:, None, :])).astype(jnp.bfloat16)
        grad_float = grad_pre.astype(jnp.float32)
        taps = []
        input_sum = jnp.zeros(inputs.shape, jnp.float32)
        for offset_row in range(3):
            for offset_col in range(3):
                taps.append(jnp.einsum('hik,hok->oi', shifted(inputs, offset_row - 1, offset_col - 1, COLS), grad_float))
                input_sum = input_sum + jnp.einsum('hok,oi->hik', shifted(grad_float, 1 - offset_row, 1 - offset_col, COLS), kernel[offset_row, offset_col])
        return (carry + jnp.stack(taps), input_sum.astype(jnp.bfloat16))
    start = jnp.zeros((9, C, C), jnp.float32)
    weight_total, grads = lax.scan(per_image, start, (feat_images, cot_images, valid_rows))
    input_grad = grads.transpose((1, 2, 0, 3)).reshape((H, C, IMAGES * COLS))
    return (input_grad, weight_total.reshape((3, 3, C, C)))
```

```python
import functools

import jax
import jax.numpy as jnp
from jax import lax
from jax.experimental import pallas as pl
from jax.experimental.pallas import tpu as pltpu
from jax.sharding import PartitionSpec as P

COLS = 128
LANES = 128
F32 = jnp.float32
BF16 = jnp.bfloat16


def kernel(
    rows_n, ch_n, split_z,
    feat, weight, cot, valid,
    in_grad, w_grad,
    xs, gs, wf, wt, cv, ig, own, sib_s, sib_r, ch_s, ch_r, z_s, z_r, fin, wout,
    loc, out_sem, xh_s, xh_r, gh_s, gh_r, ws, wr, fs, fr,
    sb_s, sb_r, cs, cr, zs_s, zs_r, ag_s, ag_r, fn_s, fn_r,
):
    band, total, cells = feat.shape
    imgs = cells // COLS
    part = weight.shape[1]
    zn = rows_n // 2
    piece = part // zn if split_z else part
    row = lax.axis_index("rows")
    chn = lax.axis_index("ch")
    core = lax.rem(row, 2)
    z = row // 2
    sib = row + 1 - 2 * core

    def ch_at(d):
        return lax.rem(chn + d, ch_n)

    def ch_from(d):
        return lax.rem(chn + ch_n - d, ch_n)

    def z_at(d):
        return lax.rem(z + d, zn)

    def z_from(d):
        return lax.rem(z + zn - d, zn)

    def remote(src, dst, send, recv, r, c):
        return pltpu.make_async_remote_copy(
            src_ref=src, dst_ref=dst, send_sem=send, recv_sem=recv,
            device_id=(r, c), device_id_type=pl.DeviceIdType.MESH,
        )

    has_up = row > 0
    has_dn = row < rows_n - 1

    l_feat = pltpu.make_async_copy(feat, xs.at[1:band + 1, total:2 * total, :], loc.at[0])
    l_cot = pltpu.make_async_copy(cot, cv, loc.at[1])
    l_w = pltpu.make_async_copy(
        weight, wf.at[:, pl.ds(pl.multiple_of(chn * part, part), part), :], loc.at[2]
    )
    l_feat.start()
    l_w.start()
    l_cot.start()

    barrier = pltpu.get_barrier_semaphore()
    for d in range(1, rows_n):
        pl.semaphore_signal(
            barrier, inc=1, device_id=(lax.rem(row + d, rows_n), chn),
            device_id_type=pl.DeviceIdType.MESH,
        )
    for d in range(1, ch_n):
        pl.semaphore_signal(
            barrier, inc=1, device_id=(row, ch_at(d)), device_id_type=pl.DeviceIdType.MESH
        )
    pl.semaphore_wait(barrier, rows_n - 1 + ch_n - 1)

    half = pl.ds(pl.multiple_of(core * LANES, LANES), LANES)
    other_half = pl.ds(pl.multiple_of((1 - core) * LANES, LANES), LANES)

    def o_slice(c):
        return pl.ds(pl.multiple_of(c * part, part), part)

    w_sends = [
        remote(weight.at[:, :, half], wf.at[:, o_slice(chn), half],
               ws.at[d - 1], wr.at[d - 1], row, ch_at(d))
        for d in range(1, ch_n)
    ]
    w_recvs = [
        remote(weight.at[:, :, half], wf.at[:, o_slice(ch_from(d)), half],
               ws.at[d - 1], wr.at[d - 1], row, ch_at(d))
        for d in range(1, ch_n)
    ]
    for copy in w_sends:
        copy.start()

    def halo(buf, source_top, source_bottom, send, recv):
        up = remote(source_top, buf.at[band + 1, total:2 * total, :],
                    send.at[0], recv.at[0], row - 1, chn)
        dn = remote(source_bottom, buf.at[0, total:2 * total, :],
                    send.at[1], recv.at[1], row + 1, chn)
        return up, dn

    x_up, x_dn = halo(xs, feat.at[0], feat.at[band - 1], xh_s, xh_r)

    def halo_start(up, dn):
        @pl.when(has_up)
        def _():
            up.start()

        @pl.when(has_dn)
        def _():
            dn.start()

    def halo_finish(buf, up, dn):
        @pl.when(has_up)
        def _():
            up.wait_send()
            dn.wait_recv()

        @pl.when(has_dn)
        def _():
            dn.wait_send()
            up.wait_recv()

        @pl.when(jnp.logical_not(has_up))
        def _():
            buf[0, total:2 * total, :] = jnp.zeros((total, cells), BF16)

        @pl.when(jnp.logical_not(has_dn))
        def _():
            buf[band + 1, total:2 * total, :] = jnp.zeros((total, cells), BF16)

    halo_start(x_up, x_dn)

    lane = lax.broadcasted_iota(jnp.int32, (total, COLS), 1)
    before, after = 0, 2 * total

    def shift_row(buf, p, minus_at, plus_at):
        for n in range(imgs):
            cols = pl.ds(n * COLS, COLS)
            v = buf[p, total:2 * total, cols].astype(F32)
            minus = jnp.where(lane == 0, 0.0, pltpu.roll(v, 1, 1))
            plus = jnp.where(lane == COLS - 1, 0.0, pltpu.roll(v, COLS - 1, 1))
            buf[p, minus_at:minus_at + total, cols] = minus.astype(BF16)
            buf[p, plus_at:plus_at + total, cols] = plus.astype(BF16)

    l_feat.wait()

    def shift_x(s, carry):
        shift_row(xs, s + 1, before, after)
        return carry

    lax.fori_loop(0, band, shift_x, 0)
    halo_finish(xs, x_up, x_dn)

    def shift_x_edge(s, carry):
        shift_row(xs, s * (band + 1), before, after)
        return carry

    lax.fori_loop(0, 2, shift_x_edge, 0)

    f_sends, f_recvs = [], []
    for d in range(1, ch_n):
        w_recvs[d - 1].wait_recv()
        here = wf.at[:, o_slice(ch_from(d)), half]
        there = wf.at[:, o_slice(ch_from(d)), other_half]
        send = remote(here, here, fs.at[d - 1], fr.at[d - 1], sib, chn)
        send.start()
        f_sends.append(send)
        f_recvs.append(remote(there, there, fs.at[d - 1], fr.at[d - 1], sib, chn))
    l_w.wait()
    l_cot.wait()
    for copy in f_recvs:
        copy.wait_recv()

    def forward(h):
        w_all = jnp.concatenate([wf[t] for t in range(9)], axis=1)
        x_all = jnp.concatenate([xs[h], xs[h + 1], xs[h + 2]], axis=0)
        summed = jnp.dot(w_all, x_all, preferred_element_type=F32)
        center = jnp.sum(summed, 0, keepdims=True) / total
        spread = jnp.sum(summed * summed, 0, keepdims=True) / total - center * center
        inverse = lax.rsqrt(spread + 1e-06)
        normed = (summed - center) * inverse
        keep = jnp.concatenate(
            [
                jnp.full((1, COLS), (row * band + h < valid[chn * imgs + n]).astype(F32))
                for n in range(imgs)
            ],
            axis=1,
        )
        masked = cv[h].astype(F32) * keep
        mean = jnp.sum(masked, 0, keepdims=True) / total
        cross = jnp.sum(masked * normed, 0, keepdims=True) / total
        gs[h + 1, total:2 * total, :] = (inverse * (masked - mean - normed * cross)).astype(BF16)

    def edge_row(s, carry):
        forward(s * (band - 1))
        return carry

    lax.fori_loop(0, 2, edge_row, 0)
    g_up, g_dn = halo(
        gs, gs.at[1, total:2 * total, :], gs.at[band, total:2 * total, :], gh_s, gh_r
    )
    halo_start(g_up, g_dn)

    def mid_row(s, carry):
        forward(s + 1)
        return carry

    lax.fori_loop(0, band - 2, mid_row, 0)

    sib_copies = []

    def weight_step(r):
        grads = jnp.concatenate([gs[h + 1, total:2 * total, :] for h in range(band)], axis=1)
        for c in range(3):
            window = jnp.concatenate(
                [xs[h + r, c * total:(c + 1) * total, :] for h in range(band)], axis=1
            )
            term = lax.dot_general(
                grads, window, (((1,), (1,)), ((), ())), preferred_element_type=F32
            )
            low, high = term[:, :LANES], term[:, LANES:]
            own[3 * r + c] = jnp.where(core == 0, low, high)
            sib_s[3 * r + c] = jnp.where(core == 0, high, low).astype(BF16)
        group = pl.ds(3 * r, 3)
        copy = remote(sib_s.at[group], sib_r.at[group], sb_s.at[r], sb_r.at[r], sib, chn)
        copy.start()
        sib_copies.append(copy)

    ch_sends = []

    def combine(g):
        sib_copies[g].wait_recv()
        for t in range(3 * g, 3 * g + 3):
            both = own[t] + sib_r[t].astype(F32)
            own[t] = both
            ch_s[t] = both.astype(BF16)
        group = pl.ds(3 * g, 3)
        for d in range(1, ch_n):
            copy = remote(
                ch_s.at[group, o_slice(ch_at(d)), :], ch_r.at[d - 1, group],
                cs.at[g, d - 1], cr.at[g, d - 1], row, ch_at(d),
            )
            copy.start()
            ch_sends.append(copy)

    z_sends = []

    def z_piece(j):
        return pl.ds(pl.multiple_of(j * piece, piece), piece) if split_z else pl.ds(0, piece)

    def plane_sum(g):
        group = pl.ds(3 * g, 3)
        for d in range(1, ch_n):
            ch_sends[g * (ch_n - 1) + d - 1].wait_recv()
        acc = own[group, o_slice(chn), :]
        for d in range(1, ch_n):
            acc = acc + ch_r[d - 1, group].astype(F32)
        z_s[group] = acc.astype(BF16)
        for d in range(1, zn):
            copy = remote(
                z_s.at[group, z_piece(z_at(d)), :], z_r.at[z, group],
                zs_s.at[g, d - 1], zs_r.at[g, d - 1], 2 * z_at(d) + core, chn,
            )
            copy.start()
            z_sends.append(copy)

    ag_sends = []

    def line_sum(g):
        group = pl.ds(3 * g, 3)
        z_r[z, group] = z_s[group, z_piece(z), :]
        for d in range(1, zn):
            src = z_s.at[group, z_piece(z_at(d)), :]
            remote(src, z_r.at[z_from(d), group], zs_s.at[g, d - 1], zs_r.at[g, d - 1],
                   2 * z_at(d) + core, chn).wait_recv()
        acc = z_r[0, group].astype(F32)
        for s in range(1, zn):
            acc = acc + z_r[s, group].astype(F32)
        fin[core, group, z_piece(z), :] = acc.astype(BF16)
        if split_z:
            mine = fin.at[core, group, z_piece(z), :]
            for d in range(1, zn):
                copy = remote(mine, mine, ag_s.at[g, d - 1], ag_r.at[g, d - 1],
                              2 * z_at(d) + core, chn)
                copy.start()
                ag_sends.append(copy)

    fin_sends = []

    def pass_on(g):
        group = pl.ds(3 * g, 3)
        if split_z:
            for d in range(1, zn):
                theirs = fin.at[core, group, z_piece(z_from(d)), :]
                remote(theirs, theirs, ag_s.at[g, d - 1], ag_r.at[g, d - 1],
                       2 * z_at(d) + core, chn).wait_recv()
        copy = remote(fin.at[core, group], fin.at[core, group],
                      fn_s.at[g], fn_r.at[g], sib, chn)
        copy.start()
        fin_sends.append(copy)

    def transpose_taps(t, carry):
        r, c = t // 3, lax.rem(t, 3)
        at = pl.multiple_of(((2 - r) * 3 + c) * total, total)
        wt[:, pl.ds(at, total)] = wf[t].T
        return carry

    def shift_g(s, carry):
        shift_row(gs, s + 1, after, before)
        return carry

    def shift_g_edge(s, carry):
        shift_row(gs, s * (band + 1), after, before)
        return carry

    out_copies = []

    def input_row(h):
        g_all = jnp.concatenate([gs[h], gs[h + 1], gs[h + 2]], axis=0)
        ig[h] = jnp.dot(wt[...], g_all, preferred_element_type=F32).astype(BF16)

    def input_out(h):
        copy = pltpu.make_async_copy(ig.at[h], in_grad.at[h], out_sem.at[h])
        copy.start()
        out_copies.append(copy)

    def input_edges(s, carry):
        input_row(s * (band - 1))
        return carry

    def input_mid(s, carry):
        input_row(s + 1)
        return carry

    weight_step(0)
    weight_step(1)
    combine(0)
    weight_step(2)
    combine(1)
    lax.fori_loop(0, 9, transpose_taps, 0)
    combine(2)
    plane_sum(0)
    lax.fori_loop(0, band, shift_g, 0)
    plane_sum(1)
    halo_finish(gs, g_up, g_dn)
    lax.fori_loop(0, 2, shift_g_edge, 0)
    plane_sum(2)
    line_sum(0)
    lax.fori_loop(0, band - 2, input_mid, 0)
    for h in range(1, band - 1):
        input_out(h)
    line_sum(1)
    line_sum(2)
    pass_on(0)
    lax.fori_loop(0, 2, input_edges, 0)
    for h in (0, band - 1):
        input_out(h)
    pass_on(1)
    pass_on(2)
    w_outs = []
    for g in range(3):
        group = pl.ds(3 * g, 3)
        remote(fin.at[core, group], fin.at[1 - core, group],
               fn_s.at[g], fn_r.at[g], sib, chn).wait_recv()
        wout[group, :, :LANES] = fin[0, group].astype(F32)
        wout[group, :, LANES:] = fin[1, group].astype(F32)
        copy = pltpu.make_async_copy(wout.at[group], w_grad.at[group], out_sem.at[band + g])
        copy.start()
        w_outs.append(copy)

    for copy in w_sends + f_sends + sib_copies + ch_sends + z_sends + ag_sends + fin_sends:
        copy.wait_send()
    for copy in out_copies + w_outs:
        copy.wait()


def body(rows_n, ch_n, features, conv_weight, cotangent, valid_rows):
    band, total, cells = features.shape
    part = conv_weight.shape[2]
    zn = rows_n // 2
    split_z = part % (16 * zn) == 0
    piece = part // zn if split_z else part
    dma = pltpu.SemaphoreType.DMA
    anywhere = pl.BlockSpec(memory_space=pl.ANY)
    in_grad, w_grad = pl.pallas_call(
        functools.partial(kernel, rows_n, ch_n, split_z),
        out_shape=(
            jax.ShapeDtypeStruct((band, total, cells), BF16),
            jax.ShapeDtypeStruct((9, part, total), F32),
        ),
        in_specs=[anywhere, anywhere, anywhere, pl.BlockSpec(memory_space=pltpu.SMEM)],
        out_specs=(anywhere, anywhere),
        scratch_shapes=[
            pltpu.VMEM((band + 2, 3 * total, cells), BF16),
            pltpu.VMEM((band + 2, 3 * total, cells), BF16),
            pltpu.VMEM((9, total, total), BF16),
            pltpu.VMEM((total, 9 * total), BF16),
            pltpu.VMEM((band, total, cells), BF16),
            pltpu.VMEM((band, total, cells), BF16),
            pltpu.VMEM((9, total, LANES), F32),
            pltpu.VMEM((9, total, LANES), BF16),
            pltpu.VMEM((9, total, LANES), BF16),
            pltpu.VMEM((9, total, LANES), BF16),
            pltpu.VMEM((ch_n - 1, 9, part, LANES), BF16),
            pltpu.VMEM((9, part, LANES), BF16),
            pltpu.VMEM((zn, 9, piece, LANES), BF16),
            pltpu.VMEM((2, 9, part, LANES), BF16),
            pltpu.VMEM((9, part, total), F32),
            dma((3,)), dma((band + 3,)),
            dma((2,)), dma((2,)), dma((2,)), dma((2,)),
            dma((ch_n - 1,)), dma((ch_n - 1,)), dma((ch_n - 1,)), dma((ch_n - 1,)),
            dma((3,)), dma((3,)),
            dma((3, ch_n - 1)), dma((3, ch_n - 1)),
            dma((3, zn - 1)), dma((3, zn - 1)),
            dma((3, zn - 1)), dma((3, zn - 1)),
            dma((3,)), dma((3,)),
        ],
        compiler_params=pltpu.CompilerParams(
            collective_id=0, has_side_effects=True, vmem_limit_bytes=56 * 1024 * 1024
        ),
        name="pyramid_backward",
    )(features, conv_weight.reshape(9, part, total), cotangent, valid_rows)
    return in_grad, w_grad.reshape(3, 3, part, total)


def solution(mesh):
    in_specs = (P("rows", None, "ch"), P(None, None, "ch", None), P("rows", None, "ch"), P())
    out_specs = (P("rows", None, "ch"), P(None, None, "ch", None))
    step = functools.partial(body, mesh.shape["rows"], mesh.shape["ch"])
    return jax.shard_map(step, mesh=mesh, in_specs=in_specs, out_specs=out_specs, check_vma=False)
```

```python
import functools

import jax
import jax.numpy as jnp
from jax import lax
from jax.experimental import pallas as pl
from jax.experimental.pallas import tpu as pltpu
from jax.sharding import PartitionSpec as P

COLS = 128
LANES = 128
F32 = jnp.float32
BF16 = jnp.bfloat16
GROUPS = [(0, 2), (2, 2), (4, 2), (6, 2), (8, 1)]


def kernel(
    rows_n, ch_n, split_z,
    feat, weight, cot, valid,
    in_grad, w_grad,
    xs, gs, wf, wt, cv, own, sib_s, sib_r, ch_s, ch_r, z_s, z_r, fin,
    loc, xh_s, xh_r, gh_s, gh_r, ws, wr, fs, fr,
    sb_s, sb_r, cs, cr, zs_s, zs_r, ag_s, ag_r, fn_s, fn_r,
):
    band, total, cells = feat.shape
    imgs = cells // COLS
    part = weight.shape[1]
    zn = rows_n // 2
    piece = part // zn if split_z else part
    row = lax.axis_index("rows")
    chn = lax.axis_index("ch")
    core = lax.rem(row, 2)
    z = row // 2
    sib = row + 1 - 2 * core

    def ch_at(d):
        return lax.rem(chn + d, ch_n)

    def ch_from(d):
        return lax.rem(chn + ch_n - d, ch_n)

    def z_at(d):
        return lax.rem(z + d, zn)

    def z_from(d):
        return lax.rem(z + zn - d, zn)

    def remote(src, dst, send, recv, r, c):
        return pltpu.make_async_remote_copy(
            src_ref=src, dst_ref=dst, send_sem=send, recv_sem=recv,
            device_id=(r, c), device_id_type=pl.DeviceIdType.MESH,
        )

    has_up = row > 0
    has_dn = row < rows_n - 1

    l_feat = pltpu.make_async_copy(feat, xs.at[1:band + 1, total:2 * total, :], loc.at[0])
    l_cot = pltpu.make_async_copy(cot, cv, loc.at[1])
    l_w = pltpu.make_async_copy(
        weight, wf.at[:, pl.ds(pl.multiple_of(chn * part, part), part), :], loc.at[2]
    )
    l_feat.start()
    l_w.start()
    l_cot.start()

    barrier = pltpu.get_barrier_semaphore()
    for d in range(1, rows_n):
        pl.semaphore_signal(
            barrier, inc=1, device_id=(lax.rem(row + d, rows_n), chn),
            device_id_type=pl.DeviceIdType.MESH,
        )
    for d in range(1, ch_n):
        pl.semaphore_signal(
            barrier, inc=1, device_id=(row, ch_at(d)), device_id_type=pl.DeviceIdType.MESH
        )
    pl.semaphore_wait(barrier, rows_n - 1 + ch_n - 1)

    half = pl.ds(pl.multiple_of(core * LANES, LANES), LANES)
    other_half = pl.ds(pl.multiple_of((1 - core) * LANES, LANES), LANES)

    def o_slice(c):
        return pl.ds(pl.multiple_of(c * part, part), part)

    w_sends = [
        remote(weight.at[:, :, half], wf.at[:, o_slice(chn), half],
               ws.at[d - 1], wr.at[d - 1], row, ch_at(d))
        for d in range(1, ch_n)
    ]
    w_recvs = [
        remote(weight.at[:, :, half], wf.at[:, o_slice(ch_from(d)), half],
               ws.at[d - 1], wr.at[d - 1], row, ch_at(d))
        for d in range(1, ch_n)
    ]
    for copy in w_sends:
        copy.start()

    def halo(buf, source_top, source_bottom, send, recv):
        up = remote(source_top, buf.at[band + 1, total:2 * total, :],
                    send.at[0], recv.at[0], row - 1, chn)
        dn = remote(source_bottom, buf.at[0, total:2 * total, :],
                    send.at[1], recv.at[1], row + 1, chn)
        return up, dn

    x_up, x_dn = halo(xs, feat.at[0], feat.at[band - 1], xh_s, xh_r)

    def halo_start(up, dn):
        @pl.when(has_up)
        def _():
            up.start()

        @pl.when(has_dn)
        def _():
            dn.start()

    def halo_finish(buf, up, dn):
        @pl.when(has_up)
        def _():
            up.wait_send()
            dn.wait_recv()

        @pl.when(has_dn)
        def _():
            dn.wait_send()
            up.wait_recv()

        @pl.when(jnp.logical_not(has_up))
        def _():
            buf[0, total:2 * total, :] = jnp.zeros((total, cells), BF16)

        @pl.when(jnp.logical_not(has_dn))
        def _():
            buf[band + 1, total:2 * total, :] = jnp.zeros((total, cells), BF16)

    halo_start(x_up, x_dn)

    lane = lax.broadcasted_iota(jnp.int32, (total, COLS), 1)
    before, after = 0, 2 * total

    def shift_row(buf, p, minus_at, plus_at):
        for n in range(imgs):
            cols = pl.ds(n * COLS, COLS)
            v = buf[p, total:2 * total, cols].astype(F32)
            minus = jnp.where(lane == 0, 0.0, pltpu.roll(v, 1, 1))
            plus = jnp.where(lane == COLS - 1, 0.0, pltpu.roll(v, COLS - 1, 1))
            buf[p, minus_at:minus_at + total, cols] = minus.astype(BF16)
            buf[p, plus_at:plus_at + total, cols] = plus.astype(BF16)

    l_feat.wait()

    def shift_x(s, carry):
        shift_row(xs, s + 1, before, after)
        return carry

    lax.fori_loop(0, band, shift_x, 0)
    halo_finish(xs, x_up, x_dn)

    def shift_x_edge(s, carry):
        shift_row(xs, s * (band + 1), before, after)
        return carry

    lax.fori_loop(0, 2, shift_x_edge, 0)

    f_sends, f_recvs = [], []
    for d in range(1, ch_n):
        w_recvs[d - 1].wait_recv()
        here = wf.at[:, o_slice(ch_from(d)), half]
        there = wf.at[:, o_slice(ch_from(d)), other_half]
        send = remote(here, here, fs.at[d - 1], fr.at[d - 1], sib, chn)
        send.start()
        f_sends.append(send)
        f_recvs.append(remote(there, there, fs.at[d - 1], fr.at[d - 1], sib, chn))
    l_w.wait()
    l_cot.wait()
    for copy in f_recvs:
        copy.wait_recv()

    def forward(h):
        w_all = jnp.concatenate([wf[t] for t in range(9)], axis=1)
        x_all = jnp.concatenate([xs[h], xs[h + 1], xs[h + 2]], axis=0)
        summed = jnp.dot(w_all, x_all, preferred_element_type=F32)
        center = jnp.sum(summed, 0, keepdims=True) / total
        spread = jnp.sum(summed * summed, 0, keepdims=True) / total - center * center
        inverse = lax.rsqrt(spread + 1e-06)
        normed = (summed - center) * inverse
        keep = jnp.concatenate(
            [
                jnp.full((1, COLS), (row * band + h < valid[chn * imgs + n]).astype(F32))
                for n in range(imgs)
            ],
            axis=1,
        )
        masked = cv[h].astype(F32) * keep
        mean = jnp.sum(masked, 0, keepdims=True) / total
        cross = jnp.sum(masked * normed, 0, keepdims=True) / total
        gs[h + 1, total:2 * total, :] = (inverse * (masked - mean - normed * cross)).astype(BF16)

    def edge_row(s, carry):
        forward(s * (band - 1))
        return carry

    lax.fori_loop(0, 2, edge_row, 0)
    g_up, g_dn = halo(
        gs, gs.at[1, total:2 * total, :], gs.at[band, total:2 * total, :], gh_s, gh_r
    )
    halo_start(g_up, g_dn)

    def mid_row(s, carry):
        forward(s + 1)
        return carry

    lax.fori_loop(0, band - 2, mid_row, 0)

    sib_copies = {}

    def weight_step(g):
        first, count = GROUPS[g]
        for t in range(first, first + count):
            r, c = divmod(t, 3)
            grads = jnp.concatenate(
                [gs[h + 1, total:2 * total, :] for h in range(band)], axis=1
            )
            window = jnp.concatenate(
                [xs[h + r, c * total:(c + 1) * total, :] for h in range(band)], axis=1
            )
            term = lax.dot_general(
                grads, window, (((1,), (1,)), ((), ())), preferred_element_type=F32
            )
            low, high = term[:, :LANES], term[:, LANES:]
            own[t] = jnp.where(core == 0, low, high)
            sib_s[t] = jnp.where(core == 0, high, low).astype(BF16)
        group = pl.ds(first, count)
        copy = remote(sib_s.at[group], sib_r.at[group], sb_s.at[g], sb_r.at[g], sib, chn)
        copy.start()
        sib_copies[g] = copy

    sends = []
    ch_copies = {}

    def combine(g):
        first, count = GROUPS[g]
        sib_copies[g].wait_recv()
        for t in range(first, first + count):
            both = own[t] + sib_r[t].astype(F32)
            own[t] = both
            ch_s[t] = both.astype(BF16)
        group = pl.ds(first, count)
        for d in range(1, ch_n):
            copy = remote(
                ch_s.at[group, o_slice(ch_at(d)), :], ch_r.at[d - 1, group],
                cs.at[g, d - 1], cr.at[g, d - 1], row, ch_at(d),
            )
            copy.start()
            sends.append(copy)
            ch_copies[g, d] = copy

    def z_piece(j):
        return pl.ds(pl.multiple_of(j * piece, piece), piece) if split_z else pl.ds(0, piece)

    def plane_sum(g):
        group = pl.ds(*GROUPS[g])
        for d in range(1, ch_n):
            ch_copies[g, d].wait_recv()
        acc = own[group, o_slice(chn), :]
        for d in range(1, ch_n):
            acc = acc + ch_r[d - 1, group].astype(F32)
        z_s[group] = acc.astype(BF16)
        for d in range(1, zn):
            copy = remote(
                z_s.at[group, z_piece(z_at(d)), :], z_r.at[z, group],
                zs_s.at[g, d - 1], zs_r.at[g, d - 1], 2 * z_at(d) + core, chn,
            )
            copy.start()
            sends.append(copy)

    def line_sum(g):
        group = pl.ds(*GROUPS[g])
        z_r[z, group] = z_s[group, z_piece(z), :]
        for d in range(1, zn):
            src = z_s.at[group, z_piece(z_at(d)), :]
            remote(src, z_r.at[z_from(d), group], zs_s.at[g, d - 1], zs_r.at[g, d - 1],
                   2 * z_at(d) + core, chn).wait_recv()
        acc = z_r[0, group].astype(F32)
        for s in range(1, zn):
            acc = acc + z_r[s, group].astype(F32)
        fin[core, group, z_piece(z), :] = acc.astype(BF16)
        if split_z:
            mine = fin.at[core, group, z_piece(z), :]
            for d in range(1, zn):
                copy = remote(mine, mine, ag_s.at[g, d - 1], ag_r.at[g, d - 1],
                              2 * z_at(d) + core, chn)
                copy.start()
                sends.append(copy)

    def pass_on(g):
        group = pl.ds(*GROUPS[g])
        if split_z:
            mine = fin.at[core, group, z_piece(z), :]
            for d in range(1, zn):
                theirs = fin.at[core, group, z_piece(z_from(d)), :]
                remote(mine, theirs, ag_s.at[g, d - 1], ag_r.at[g, d - 1],
                       2 * z_at(d) + core, chn).wait_recv()
        both = fin.at[core, group]
        copy = remote(both, both, fn_s.at[g], fn_r.at[g], sib, chn)
        copy.start()
        sends.append(copy)

    def finish(g):
        group = pl.ds(*GROUPS[g])
        remote(fin.at[core, group], fin.at[1 - core, group],
               fn_s.at[g], fn_r.at[g], sib, chn).wait_recv()
        w_grad[group, :, :LANES] = fin[0, group].astype(F32)
        w_grad[group, :, LANES:] = fin[1, group].astype(F32)

    def transpose_taps(t, carry):
        r, c = t // 3, lax.rem(t, 3)
        at = pl.multiple_of(((2 - r) * 3 + c) * total, total)
        wt[:, pl.ds(at, total)] = wf[t].T
        return carry

    def shift_g(s, carry):
        shift_row(gs, s + 1, after, before)
        return carry

    def shift_g_edge(s, carry):
        shift_row(gs, s * (band + 1), after, before)
        return carry

    def input_row(h, carry):
        g_all = jnp.concatenate([gs[h], gs[h + 1], gs[h + 2]], axis=0)
        in_grad[h] = jnp.dot(wt[...], g_all, preferred_element_type=F32).astype(BF16)
        return carry

    def edges_in():
        halo_finish(gs, g_up, g_dn)
        lax.fori_loop(0, 2, shift_g_edge, 0)

    fill = [(0.3 * count, functools.partial(weight_step, g))
            for g, (_, count) in enumerate(GROUPS)]
    fill.append((0.8, lambda: lax.fori_loop(0, 9, transpose_taps, 0)))
    fill.append((0.8, lambda: lax.fori_loop(0, band, shift_g, 0)))
    for h in range(1, band - 1):
        fill.append((0.8, functools.partial(input_row, h, 0)))
    fill.append((0.4, edges_in))
    for h in (0, band - 1):
        fill.append((0.8, functools.partial(input_row, h, 0)))
    events = []
    ready, wire = 0.0, 0.0
    for g, (_, count) in enumerate(GROUPS):
        ready = ready + 0.3 * count
        at = ready + 0.5
        events.append((at, g, combine))
        wire = max(wire, at) + 0.7 * count
        events.append((wire + 1.6, g, plane_sum))
        events.append((wire + 6.0, g, line_sum))
        events.append((wire + 10.4, g, pass_on))
        events.append((wire + 11.8, g, finish))
    events.sort(key=lambda e: e[:2])
    now, done = 0.0, 0
    while events or fill:
        waits = events and events[0][2] is combine and events[0][1] >= done
        if fill and (not events or waits or events[0][0] > now):
            spent, step = fill.pop(0)
            step()
            done += 1
            now += spent if done <= len(GROUPS) else spent * 1.0
        else:
            at, g, event = events.pop(0)
            event(g)
            now = max(now, at)

    for copy in w_sends + f_sends + list(sib_copies.values()) + sends:
        copy.wait_send()


def body(rows_n, ch_n, features, conv_weight, cotangent, valid_rows):
    band, total, cells = features.shape
    part = conv_weight.shape[2]
    zn = rows_n // 2
    split_z = part % (16 * zn) == 0
    piece = part // zn if split_z else part
    groups = len(GROUPS)
    dma = pltpu.SemaphoreType.DMA
    anywhere = pl.BlockSpec(memory_space=pl.ANY)
    in_grad, w_grad = pl.pallas_call(
        functools.partial(kernel, rows_n, ch_n, split_z),
        out_shape=(
            pltpu.VMEM((band, total, cells), BF16),
            pltpu.VMEM((9, part, total), F32),
        ),
        in_specs=[anywhere, anywhere, anywhere, pl.BlockSpec(memory_space=pltpu.SMEM)],
        out_specs=(pl.BlockSpec(memory_space=pltpu.VMEM),) * 2,
        scratch_shapes=[
            pltpu.VMEM((band + 2, 3 * total, cells), BF16),
            pltpu.VMEM((band + 2, 3 * total, cells), BF16),
            pltpu.VMEM((9, total, total), BF16),
            pltpu.VMEM((total, 9 * total), BF16),
            pltpu.VMEM((band, total, cells), BF16),
            pltpu.VMEM((9, total, LANES), F32),
            pltpu.VMEM((9, total, LANES), BF16),
            pltpu.VMEM((9, total, LANES), BF16),
            pltpu.VMEM((9, total, LANES), BF16),
            pltpu.VMEM((ch_n - 1, 9, part, LANES), BF16),
            pltpu.VMEM((9, part, LANES), BF16),
            pltpu.VMEM((zn, 9, piece, LANES), BF16),
            pltpu.VMEM((2, 9, part, LANES), BF16),
            dma((3,)),
            dma((2,)), dma((2,)), dma((2,)), dma((2,)),
            dma((ch_n - 1,)), dma((ch_n - 1,)), dma((ch_n - 1,)), dma((ch_n - 1,)),
            dma((groups,)), dma((groups,)),
            dma((groups, ch_n - 1)), dma((groups, ch_n - 1)),
            dma((groups, zn - 1)), dma((groups, zn - 1)),
            dma((groups, zn - 1)), dma((groups, zn - 1)),
            dma((groups,)), dma((groups,)),
        ],
        compiler_params=pltpu.CompilerParams(
            collective_id=0, has_side_effects=True, vmem_limit_bytes=56 * 1024 * 1024
        ),
        name="pyramid_backward",
    )(features, conv_weight.reshape(9, part, total), cotangent, valid_rows)
    return in_grad, w_grad.reshape(3, 3, part, total)


def solution(mesh):
    in_specs = (P("rows", None, "ch"), P(None, None, "ch", None), P("rows", None, "ch"), P())
    out_specs = (P("rows", None, "ch"), P(None, None, "ch", None))
    step = functools.partial(body, mesh.shape["rows"], mesh.shape["ch"])
    return jax.shard_map(step, mesh=mesh, in_specs=in_specs, out_specs=out_specs, check_vma=False)
```

```python
import functools

import jax
import jax.numpy as jnp
from jax import lax
from jax.experimental import pallas as pl
from jax.experimental.pallas import tpu as pltpu
from jax.sharding import PartitionSpec as P

COLS = 128
LANES = 128
F32 = jnp.float32
BF16 = jnp.bfloat16
GROUPS = [(0, 2), (2, 2), (4, 2), (6, 2), (8, 1)]


def kernel(
    rows_n, ch_n, split_z,
    feat, weight, cot, valid,
    in_grad, w_grad,
    xs, gs, wf, wt, cv, own, sib_s, sib_r, ch_s, ch_r, z_s, z_r, fin,
    loc, xh_s, xh_r, gh_s, gh_r, ws, wr, fs, fr,
    sb_s, sb_r, cs, cr, zs_s, zs_r, ag_s, ag_r, fn_s, fn_r,
):
    band, total, cells = feat.shape
    imgs = cells // COLS
    part = weight.shape[1]
    zn = rows_n // 2
    piece = part // zn if split_z else part
    row = lax.axis_index("rows")
    chn = lax.axis_index("ch")
    core = lax.rem(row, 2)
    z = row // 2
    sib = row + 1 - 2 * core

    def ch_at(d):
        return lax.rem(chn + d, ch_n)

    def ch_from(d):
        return lax.rem(chn + ch_n - d, ch_n)

    def z_at(d):
        return lax.rem(z + d, zn)

    def z_from(d):
        return lax.rem(z + zn - d, zn)

    def remote(src, dst, send, recv, r, c):
        return pltpu.make_async_remote_copy(
            src_ref=src, dst_ref=dst, send_sem=send, recv_sem=recv,
            device_id=(r, c), device_id_type=pl.DeviceIdType.MESH,
        )

    has_up = row > 0
    has_dn = row < rows_n - 1

    l_feat = pltpu.make_async_copy(feat, xs.at[1:band + 1, total:2 * total, :], loc.at[0])
    l_cot = pltpu.make_async_copy(cot, cv, loc.at[1])
    l_w = pltpu.make_async_copy(
        weight, wf.at[:, pl.ds(pl.multiple_of(chn * part, part), part), :], loc.at[2]
    )
    lane = lax.broadcasted_iota(jnp.int32, (total, COLS), 1)
    before, after = 0, 2 * total

    def shift_row(buf, p, minus_at, plus_at):
        for n in range(imgs):
            cols = pl.ds(n * COLS, COLS)
            v = buf[p, total:2 * total, cols].astype(F32)
            minus = jnp.where(lane == 0, 0.0, pltpu.roll(v, 1, 1))
            plus = jnp.where(lane == COLS - 1, 0.0, pltpu.roll(v, COLS - 1, 1))
            buf[p, minus_at:minus_at + total, cols] = minus.astype(BF16)
            buf[p, plus_at:plus_at + total, cols] = plus.astype(BF16)

    def shift_x(s, carry):
        shift_row(xs, s + 1, before, after)
        return carry

    barrier = pltpu.get_barrier_semaphore()
    for d in range(1, rows_n):
        pl.semaphore_signal(
            barrier, inc=1, device_id=(lax.rem(row + d, rows_n), chn),
            device_id_type=pl.DeviceIdType.MESH,
        )
    for d in range(1, ch_n):
        pl.semaphore_signal(
            barrier, inc=1, device_id=(row, ch_at(d)), device_id_type=pl.DeviceIdType.MESH
        )
    l_feat.start()
    l_w.start()
    l_cot.start()
    l_feat.wait()
    lax.fori_loop(0, band, shift_x, 0)
    pl.semaphore_wait(barrier, rows_n - 1 + ch_n - 1)

    half = pl.ds(pl.multiple_of(core * LANES, LANES), LANES)
    other_half = pl.ds(pl.multiple_of((1 - core) * LANES, LANES), LANES)

    def o_slice(c):
        return pl.ds(pl.multiple_of(c * part, part), part)

    w_sends = [
        remote(weight.at[:, :, half], wf.at[:, o_slice(chn), half],
               ws.at[d - 1], wr.at[d - 1], row, ch_at(d))
        for d in range(1, ch_n)
    ]
    w_recvs = [
        remote(weight.at[:, :, half], wf.at[:, o_slice(ch_from(d)), half],
               ws.at[d - 1], wr.at[d - 1], row, ch_at(d))
        for d in range(1, ch_n)
    ]
    for copy in w_sends:
        copy.start()

    def halo(buf, source_top, source_bottom, send, recv):
        up = remote(source_top, buf.at[band + 1, total:2 * total, :],
                    send.at[0], recv.at[0], row - 1, chn)
        dn = remote(source_bottom, buf.at[0, total:2 * total, :],
                    send.at[1], recv.at[1], row + 1, chn)
        return up, dn

    x_up, x_dn = halo(xs, feat.at[0], feat.at[band - 1], xh_s, xh_r)

    def halo_start(up, dn):
        @pl.when(has_up)
        def _():
            up.start()

        @pl.when(has_dn)
        def _():
            dn.start()

    def halo_finish(buf, up, dn):
        @pl.when(has_up)
        def _():
            up.wait_send()
            dn.wait_recv()

        @pl.when(has_dn)
        def _():
            dn.wait_send()
            up.wait_recv()

        @pl.when(jnp.logical_not(has_up))
        def _():
            buf[0, total:2 * total, :] = jnp.zeros((total, cells), BF16)

        @pl.when(jnp.logical_not(has_dn))
        def _():
            buf[band + 1, total:2 * total, :] = jnp.zeros((total, cells), BF16)

    halo_start(x_up, x_dn)

    halo_finish(xs, x_up, x_dn)

    def shift_x_edge(s, carry):
        shift_row(xs, s * (band + 1), before, after)
        return carry

    lax.fori_loop(0, 2, shift_x_edge, 0)

    f_sends, f_recvs = [], []
    for d in range(1, ch_n):
        w_recvs[d - 1].wait_recv()
        here = wf.at[:, o_slice(ch_from(d)), half]
        there = wf.at[:, o_slice(ch_from(d)), other_half]
        send = remote(here, here, fs.at[d - 1], fr.at[d - 1], sib, chn)
        send.start()
        f_sends.append(send)
        f_recvs.append(remote(there, there, fs.at[d - 1], fr.at[d - 1], sib, chn))
    l_w.wait()
    l_cot.wait()
    for copy in f_recvs:
        copy.wait_recv()

    def forward(h):
        w_all = jnp.concatenate([wf[t] for t in range(9)], axis=1)
        x_all = jnp.concatenate([xs[h], xs[h + 1], xs[h + 2]], axis=0)
        summed = jnp.dot(w_all, x_all, preferred_element_type=F32)
        center = jnp.sum(summed, 0, keepdims=True) / total
        spread = jnp.sum(summed * summed, 0, keepdims=True) / total - center * center
        inverse = lax.rsqrt(spread + 1e-06)
        normed = (summed - center) * inverse
        keep = jnp.concatenate(
            [
                jnp.full((1, COLS), (row * band + h < valid[chn * imgs + n]).astype(F32))
                for n in range(imgs)
            ],
            axis=1,
        )
        masked = cv[h].astype(F32) * keep
        mean = jnp.sum(masked, 0, keepdims=True) / total
        cross = jnp.sum(masked * normed, 0, keepdims=True) / total
        gs[h + 1, total:2 * total, :] = (inverse * (masked - mean - normed * cross)).astype(BF16)

    def edge_row(s, carry):
        forward(s * (band - 1))
        return carry

    lax.fori_loop(0, 2, edge_row, 0)
    g_up, g_dn = halo(
        gs, gs.at[1, total:2 * total, :], gs.at[band, total:2 * total, :], gh_s, gh_r
    )
    halo_start(g_up, g_dn)

    def mid_row(s, carry):
        forward(s + 1)
        return carry

    lax.fori_loop(0, band - 2, mid_row, 0)

    sib_copies = {}

    def weight_step(g):
        first, count = GROUPS[g]
        for t in range(first, first + count):
            r, c = divmod(t, 3)
            grads = jnp.concatenate(
                [gs[h + 1, total:2 * total, :] for h in range(band)], axis=1
            )
            window = jnp.concatenate(
                [xs[h + r, c * total:(c + 1) * total, :] for h in range(band)], axis=1
            )
            term = lax.dot_general(
                grads, window, (((1,), (1,)), ((), ())), preferred_element_type=F32
            )
            low, high = term[:, :LANES], term[:, LANES:]
            own[t] = jnp.where(core == 0, low, high)
            sib_s[t] = jnp.where(core == 0, high, low).astype(BF16)
        group = pl.ds(first, count)
        copy = remote(sib_s.at[group], sib_r.at[group], sb_s.at[g], sb_r.at[g], sib, chn)
        copy.start()
        sib_copies[g] = copy

    sends = []
    ch_copies = {}

    def combine(g):
        first, count = GROUPS[g]
        sib_copies[g].wait_recv()
        for t in range(first, first + count):
            both = own[t] + sib_r[t].astype(F32)
            own[t] = both
            ch_s[t] = both.astype(BF16)
        group = pl.ds(first, count)
        for d in range(1, ch_n):
            copy = remote(
                ch_s.at[group, o_slice(ch_at(d)), :], ch_r.at[d - 1, group],
                cs.at[g, d - 1], cr.at[g, d - 1], row, ch_at(d),
            )
            copy.start()
            sends.append(copy)
            ch_copies[g, d] = copy

    def z_piece(j):
        return pl.ds(pl.multiple_of(j * piece, piece), piece) if split_z else pl.ds(0, piece)

    def plane_sum(g):
        group = pl.ds(*GROUPS[g])
        for d in range(1, ch_n):
            ch_copies[g, d].wait_recv()
        acc = own[group, o_slice(chn), :]
        for d in range(1, ch_n):
            acc = acc + ch_r[d - 1, group].astype(F32)
        z_s[group] = acc.astype(BF16)
        for d in range(1, zn):
            copy = remote(
                z_s.at[group, z_piece(z_at(d)), :], z_r.at[z, group],
                zs_s.at[g, d - 1], zs_r.at[g, d - 1], 2 * z_at(d) + core, chn,
            )
            copy.start()
            sends.append(copy)

    def line_sum(g):
        group = pl.ds(*GROUPS[g])
        z_r[z, group] = z_s[group, z_piece(z), :]
        for d in range(1, zn):
            src = z_s.at[group, z_piece(z_at(d)), :]
            remote(src, z_r.at[z_from(d), group], zs_s.at[g, d - 1], zs_r.at[g, d - 1],
                   2 * z_at(d) + core, chn).wait_recv()
        acc = z_r[0, group].astype(F32)
        for s in range(1, zn):
            acc = acc + z_r[s, group].astype(F32)
        fin[core, group, z_piece(z), :] = acc.astype(BF16)
        if split_z:
            mine = fin.at[core, group, z_piece(z), :]
            for d in range(1, zn):
                copy = remote(mine, mine, ag_s.at[g, d - 1], ag_r.at[g, d - 1],
                              2 * z_at(d) + core, chn)
                copy.start()
                sends.append(copy)

    def pass_on(g):
        group = pl.ds(*GROUPS[g])
        if split_z:
            mine = fin.at[core, group, z_piece(z), :]
            for d in range(1, zn):
                theirs = fin.at[core, group, z_piece(z_from(d)), :]
                remote(mine, theirs, ag_s.at[g, d - 1], ag_r.at[g, d - 1],
                       2 * z_at(d) + core, chn).wait_recv()
        both = fin.at[core, group]
        copy = remote(both, both, fn_s.at[g], fn_r.at[g], sib, chn)
        copy.start()
        sends.append(copy)

    def finish(g):
        group = pl.ds(*GROUPS[g])
        remote(fin.at[core, group], fin.at[1 - core, group],
               fn_s.at[g], fn_r.at[g], sib, chn).wait_recv()
        w_grad[group, :, :LANES] = fin[0, group].astype(F32)
        w_grad[group, :, LANES:] = fin[1, group].astype(F32)

    def transpose_taps(t, carry):
        r, c = t // 3, lax.rem(t, 3)
        at = pl.multiple_of(((2 - r) * 3 + c) * total, total)
        wt[:, pl.ds(at, total)] = wf[t].T
        return carry

    def shift_g(s, carry):
        shift_row(gs, s + 1, after, before)
        return carry

    def shift_g_edge(s, carry):
        shift_row(gs, s * (band + 1), after, before)
        return carry

    def input_row(h, carry):
        g_all = jnp.concatenate([gs[h], gs[h + 1], gs[h + 2]], axis=0)
        in_grad[h] = jnp.dot(wt[...], g_all, preferred_element_type=F32).astype(BF16)
        return carry

    def edges_in():
        halo_finish(gs, g_up, g_dn)
        lax.fori_loop(0, 2, shift_g_edge, 0)

    fill = [(0.3 * count, functools.partial(weight_step, g))
            for g, (_, count) in enumerate(GROUPS)]
    fill.append((0.8, lambda: lax.fori_loop(0, 9, transpose_taps, 0)))
    fill.append((0.8, lambda: lax.fori_loop(0, band, shift_g, 0)))
    for h in range(1, band - 1):
        fill.append((0.8, functools.partial(input_row, h, 0)))
    fill.append((0.4, edges_in))
    for h in (0, band - 1):
        fill.append((0.8, functools.partial(input_row, h, 0)))
    events = []
    ready, wire = 0.0, 0.0
    for g, (_, count) in enumerate(GROUPS):
        ready = ready + 0.3 * count
        at = ready + 0.5
        events.append((at, g, combine))
        wire = max(wire, at) + 0.7 * count
        events.append((wire + 1.6, g, plane_sum))
        events.append((wire + 6.0, g, line_sum))
        events.append((wire + 10.4, g, pass_on))
        events.append((wire + 11.8, g, finish))
    events.sort(key=lambda e: e[:2])
    now, done = 0.0, 0
    while events or fill:
        waits = events and events[0][2] is combine and events[0][1] >= done
        if fill and (not events or waits or events[0][0] > now):
            spent, step = fill.pop(0)
            step()
            done += 1
            now += spent if done <= len(GROUPS) else spent * 1.0
        else:
            at, g, event = events.pop(0)
            event(g)
            now = max(now, at)

    for copy in w_sends + f_sends + list(sib_copies.values()) + sends:
        copy.wait_send()


def body(rows_n, ch_n, features, conv_weight, cotangent, valid_rows):
    band, total, cells = features.shape
    part = conv_weight.shape[2]
    zn = rows_n // 2
    split_z = part % (16 * zn) == 0
    piece = part // zn if split_z else part
    groups = len(GROUPS)
    dma = pltpu.SemaphoreType.DMA
    anywhere = pl.BlockSpec(memory_space=pl.ANY)
    in_grad, w_grad = pl.pallas_call(
        functools.partial(kernel, rows_n, ch_n, split_z),
        out_shape=(
            pltpu.VMEM((band, total, cells), BF16),
            pltpu.VMEM((9, part, total), F32),
        ),
        in_specs=[anywhere, anywhere, anywhere, pl.BlockSpec(memory_space=pltpu.SMEM)],
        out_specs=(pl.BlockSpec(memory_space=pltpu.VMEM),) * 2,
        scratch_shapes=[
            pltpu.VMEM((band + 2, 3 * total, cells), BF16),
            pltpu.VMEM((band + 2, 3 * total, cells), BF16),
            pltpu.VMEM((9, total, total), BF16),
            pltpu.VMEM((total, 9 * total), BF16),
            pltpu.VMEM((band, total, cells), BF16),
            pltpu.VMEM((9, total, LANES), F32),
            pltpu.VMEM((9, total, LANES), BF16),
            pltpu.VMEM((9, total, LANES), BF16),
            pltpu.VMEM((9, total, LANES), BF16),
            pltpu.VMEM((ch_n - 1, 9, part, LANES), BF16),
            pltpu.VMEM((9, part, LANES), BF16),
            pltpu.VMEM((zn, 9, piece, LANES), BF16),
            pltpu.VMEM((2, 9, part, LANES), BF16),
            dma((3,)),
            dma((2,)), dma((2,)), dma((2,)), dma((2,)),
            dma((ch_n - 1,)), dma((ch_n - 1,)), dma((ch_n - 1,)), dma((ch_n - 1,)),
            dma((groups,)), dma((groups,)),
            dma((groups, ch_n - 1)), dma((groups, ch_n - 1)),
            dma((groups, zn - 1)), dma((groups, zn - 1)),
            dma((groups, zn - 1)), dma((groups, zn - 1)),
            dma((groups,)), dma((groups,)),
        ],
        compiler_params=pltpu.CompilerParams(
            collective_id=0, has_side_effects=True, vmem_limit_bytes=56 * 1024 * 1024
        ),
        name="pyramid_backward",
    )(features, conv_weight.reshape(9, part, total), cotangent, valid_rows)
    return in_grad, w_grad.reshape(3, 3, part, total)


def solution(mesh):
    in_specs = (P("rows", None, "ch"), P(None, None, "ch", None), P("rows", None, "ch"), P())
    out_specs = (P("rows", None, "ch"), P(None, None, "ch", None))
    step = functools.partial(body, mesh.shape["rows"], mesh.shape["ch"])
    return jax.shard_map(step, mesh=mesh, in_specs=in_specs, out_specs=out_specs, check_vma=False)
```
